32 devices in a mesh: strip: 2 (over x), row: 16 (over z, y, core).
Axes of the slice: x: 2, y: 2, z: 4, core: 2. Of those that a mesh axis runs over, the one named last changes fastest.
Arguments:
- mask: float32 [512, 256], P(('strip', 'row')), parts along dimension 0, may hold values from 0 to 1
- target: float32 [512, 256], P(('strip', 'row')), parts along dimension 0, may hold values from 0 to 1
- kernels: bfloat16 [9, 24, 17, 17], replicated, may hold values from -0.375 to 0.375
- corner_weights: float32 [9, 12], replicated, may hold values from 0.03 to 0.3
- hotspots: int32 [32, 5], P('strip'), parts along dimension 0, may hold values from 0 to 8, as said below
- counts: int32 [32], P('strip'), parts along dimension 0, may hold values from 1 to 5, as said below
Outputs:
- updated_mask: float32 [512, 256], P(('strip', 'row')), parts along dimension 0
The draws below stay inside these ranges and needn't reach their ends.
There are 2 independent parts, one for each index of `strip`. The reference program is written for one: setup_inputs(seed, part) draws one part's arguments, and reference() takes and returns one part's arrays. A program takes and returns all parts, laid end to end along the dimension named above; an argument that names none is the same for every part. Nothing has to cross between parts.
Inputs may be any that keep to these rules, and one draw needn't show every extreme that they name: `hotspots`: each row names 5 distinct corners. `counts`: some tile has 5 in every draw; tiles t and t xor (8) together use at most 6 corners, and some such pair reaches it in every draw.
All inputs are finite; a program needn't handle non-finite values.
Results may differ from the reference program's by a relative error of at most 0.0062.
Values may be sent and summed in bfloat16 or wider, within the bound.
A program may use at most 64 MiB of HBM per device.

```python
import math
import jax
import jax.numpy as jnp
from jax import lax

K = 12
KS = 17
CORNERS = 9
SLOTS = 5
ITERS = 2
TR = 16
W = 256
NX = 256
N_ROW = 16


def draw_hotspots(key, part):
    keys = jax.random.split(jax.random.fold_in(key, 11), N_ROW)
    rows = jax.vmap(lambda row_key: jax.random.permutation(row_key, CORNERS)[:SLOTS])(keys)
    return rows.astype(jnp.int32)


def draw_counts(key, part):
    base = jax.random.fold_in(key, 23)
    half = N_ROW // 2
    heavy = jax.random.randint(jax.random.fold_in(base, 1), (half,), 0, 2) == 0
    place = jax.random.randint(jax.random.fold_in(base, 3), (), 0, half)
    heavy = heavy.at[place].set(True)
    side = jax.random.randint(jax.random.fold_in(base, 4), (half,), 0, 2)
    low_light = jax.random.randint(jax.random.fold_in(base, 2), (half,), 1, 4)
    high_light = jax.random.randint(jax.random.fold_in(base, 5), (half,), 1, 4)
    low = jnp.where(heavy, jnp.where(side == 0, SLOTS, 1), low_light)
    high = jnp.where(heavy, jnp.where(side == 0, 1, SLOTS), high_light)
    return jnp.concatenate([low, high]).astype(jnp.int32)


def shard_levels(key, shape, cuts, low, largest):
    gain, own = 1.0, jax.random.fold_in(key, 6)
    for position, shards_of in cuts:
        draws = jnp.exp(jax.random.uniform(jax.random.fold_in(own, position), (shards_of,), jnp.float32, low / len(cuts), largest / len(cuts)))
        gain = gain * jnp.repeat(draws, shape[position] // shards_of).reshape([-1 if axis == position else 1 for axis in range(len(shape))])
    return gain


def noise(key, extent, deviation, most, held_as=jnp.bfloat16):
    drawn = jax.random.normal(key, extent, jnp.float32) * deviation
    return jnp.minimum(jnp.maximum(drawn, -most), most).astype(held_as)


def setup_inputs(seed: int = 0, part: int = 0) -> dict:
    arg_keys = jax.random.split(jax.random.key(seed), 7)
    own_keys = jax.random.split(jax.random.fold_in(arg_keys[6], part), 7)
    return {
        "mask": jnp.clip(1.0 * jax.random.uniform(own_keys[0], (NX, W), jnp.float32) ** shard_levels(own_keys[0], (NX, W), ((0, 16),), -0.2, 0.2), 0.0, 1.0),
        "target": jnp.clip(1.0 * jax.random.uniform(own_keys[1], (NX, W), jnp.float32) ** shard_levels(own_keys[1], (NX, W), ((0, 16),), -0.2, 0.2), 0.0, 1.0),
        "kernels": noise(arg_keys[2], (CORNERS, 2 * K, KS, KS), (KS * KS) ** -0.5, 0.375),
        "corner_weights": jnp.clip(jnp.exp(jax.random.uniform(arg_keys[3], (CORNERS, K), jnp.float32, math.log(0.03), math.log(0.3))), 0.03, 0.3),
        "hotspots": draw_hotspots(jax.random.fold_in(jax.random.fold_in(arg_keys[6], part), 71), part),
        "counts": draw_counts(jax.random.fold_in(jax.random.fold_in(arg_keys[6], part), 71), part),
    }


steepness = 4.0
threshold = 0.8
step_rate = 1.0


def corner_term(extended, target_tile, kernel_set, weights):
    radius = kernel_set.shape[-1] // 2
    width = target_tile.shape[1]
    padded = jnp.pad(extended, ((0, 0), (radius, radius))).astype(jnp.bfloat16)
    field = lax.conv_general_dilated(padded[None, None], kernel_set[:, None], (1, 1), "VALID", dimension_numbers=("NCHW", "OIHW", "NCHW"), preferred_element_type=jnp.float32)[0]
    weight_both = jnp.concatenate([weights, weights])[:, None, None]
    intensity = jnp.sum(weight_both * field * field, axis=0)
    resist = jax.nn.sigmoid(steepness * (intensity - threshold))
    slope = 2.0 * (resist - target_tile) * steepness * resist * (1.0 - resist)
    source = (2.0 * weight_both * slope[None] * field).astype(jnp.bfloat16)
    flipped = kernel_set[None, :, ::-1, ::-1]
    span = 2 * radius
    back = lax.conv_general_dilated(source[None], flipped, (1, 1), ((span, span), (span, span)), dimension_numbers=("NCHW", "OIHW", "NCHW"), preferred_element_type=jnp.float32)[0, 0]
    return back[:, radius:radius + width]


def reference(mask, target, kernels, corner_weights, hotspots, counts):
    radius = KS // 2
    field = mask
    for step in range(ITERS):
        padded = jnp.pad(field, ((radius, radius), (0, 0)))

        def tile_fn(tile, grad_pad):
            tile = jnp.asarray(tile).astype(jnp.int32)
            start = (tile * TR).astype(jnp.int32)
            extended = lax.dynamic_slice_in_dim(padded, start, TR + 2 * radius, 0)
            target_tile = lax.dynamic_slice_in_dim(target, start, TR, 0)

            def corner_fn(slot, total):
                corner = hotspots[tile, slot]
                return total + corner_term(extended, target_tile, kernels[corner], corner_weights[corner])

            zeros = jnp.zeros((TR + 2 * radius, W), jnp.float32)
            total = lax.fori_loop(jnp.int32(0), counts[tile].astype(jnp.int32), corner_fn, zeros)
            previous = lax.dynamic_slice_in_dim(grad_pad, start, TR + 2 * radius, 0)
            return lax.dynamic_update_slice_in_dim(grad_pad, previous + total, start, 0)

        grad_pad = lax.fori_loop(0, N_ROW, tile_fn, jnp.zeros((NX + 2 * radius, W), jnp.float32))
        field = field - step_rate * grad_pad[radius:radius + NX]
    return field
```

```python
import functools

import jax
import jax.numpy as jnp
from jax import lax
from jax.experimental import pallas as pl
from jax.experimental.pallas import tpu as pltpu
from jax.sharding import PartitionSpec as P

ITERS = 2
STEEPNESS = 4.0
THRESHOLD = 0.8
STEP_RATE = 1.0
LANES = 128
MESH = pl.DeviceIdType.MESH


def cdiv(a, b):
    return -(-a // b)


def round_up(a, b):
    return cdiv(a, b) * b


class Plan:
    def __init__(self, rows, width, channels, side, slots):
        self.rows, self.width, self.channels = rows, width, channels
        self.side, self.slots = side, slots
        self.radius = side // 2
        self.groups = rows // self.radius
        self.ext = rows + 2 * self.radius
        self.window = 3 * self.radius
        self.per = LANES // self.window
        self.stretches = cdiv(side, self.per)
        self.depth = self.stretches * LANES
        self.used = round_up(self.offset(side - 1) + self.window, 16)
        self.slot_rows = channels * self.radius
        self.mix = round_up(slots * self.slot_rows, 256)

    def offset(self, b):
        return (b // self.per) * LANES + (b % self.per) * self.window


def shifted(value, by):
    width = value.shape[1]
    if by == 0:
        return value
    moved = pltpu.roll(value, by % width, 1)
    column = lax.broadcasted_iota(jnp.int32, value.shape, 1)
    keep = column >= by if by > 0 else column < width + by
    return jnp.where(keep, moved, 0.0)


def kernel(p, devices, hot_ref, count_ref, weight_ref, mask_ref, target_ref, base_ref, out_ref,
           big, big_t, patches, source, field, total, halo, got, send_sem, recv_sem):
    me = lax.axis_index("row")
    r = p.radius
    has_up, has_down = me > 0, me < devices - 1
    kinds = weight_ref.shape[1]

    barrier = pltpu.get_barrier_semaphore()

    @pl.when(has_up)
    def _():
        pl.semaphore_signal(barrier, inc=1, device_id={"row": me - 1}, device_id_type=MESH)

    @pl.when(has_down)
    def _():
        pl.semaphore_signal(barrier, inc=1, device_id={"row": me + 1}, device_id_type=MESH)

    def copies(stage, up_src, down_src, above, below):
        up = pltpu.make_async_remote_copy(
            src_ref=up_src, dst_ref=below, send_sem=send_sem.at[stage, 0],
            recv_sem=recv_sem.at[stage, 0], device_id={"row": me - 1}, device_id_type=MESH)
        down = pltpu.make_async_remote_copy(
            src_ref=down_src, dst_ref=above, send_sem=send_sem.at[stage, 1],
            recv_sem=recv_sem.at[stage, 1], device_id={"row": me + 1}, device_id_type=MESH)
        return up, down

    def start(pair):
        up, down = pair

        @pl.when(has_up)
        def _():
            up.start()

        @pl.when(has_down)
        def _():
            down.start()

    def finish(pair):
        up, down = pair

        @pl.when(has_up)
        def _():
            up.wait_send()
            down.wait_recv()

        @pl.when(has_down)
        def _():
            down.wait_send()
            up.wait_recv()

    @pl.when(jnp.logical_not(has_up))
    def _():
        halo[0] = jnp.zeros(halo.shape[1:], halo.dtype)
        for step in range(ITERS):
            got[step, 0] = jnp.zeros(got.shape[2:], got.dtype)

    @pl.when(jnp.logical_not(has_down))
    def _():
        halo[1] = jnp.zeros(halo.shape[1:], halo.dtype)
        for step in range(ITERS):
            got[step, 1] = jnp.zeros(got.shape[2:], got.dtype)

    inner = has_up & has_down

    @pl.when(inner)
    def _():
        pl.semaphore_wait(barrier, 2)

    @pl.when(jnp.logical_not(inner))
    def _():
        pl.semaphore_wait(barrier, 1)

    first = copies(0, mask_ref.at[pl.ds(0, r)], mask_ref.at[pl.ds(p.rows - r, r)],
                   halo.at[0], halo.at[1])
    start(first)

    corners = [hot_ref[me, s] for s in range(p.slots)]
    count = count_ref[me]
    for s in range(p.slots):
        base = base_ref[corners[s]]
        for q in range(p.stretches):
            part = base[:, q * LANES : (q + 1) * LANES]
            wide = jnp.broadcast_to(part[:, None, :], (p.channels, r, LANES))
            turned = pltpu.roll(wide, 0, 2, stride=1, stride_axis=1)
            flat = turned.reshape(p.slot_rows, LANES)
            big[pl.ds(s * p.slot_rows, p.slot_rows), pl.ds(q * LANES, LANES)] = flat
    rest = p.mix - p.slots * p.slot_rows
    if rest:
        big[pl.ds(p.slots * p.slot_rows, rest), :] = jnp.zeros((rest, p.depth), jnp.float32)
        source[pl.ds(p.slots * p.slot_rows, rest), :] = jnp.zeros((rest, source.shape[1]), jnp.bfloat16)
    for q in range(p.mix // 256):
        big_t[:, pl.ds(q * 256, 256)] = big[pl.ds(q * 256, 256), :].T.astype(jnp.bfloat16)

    target = jnp.concatenate([target_ref[pl.ds(g * r, r), :] for g in range(p.groups)], axis=1)
    finish(first)
    field[pl.ds(0, r), :] = halo[0]
    field[pl.ds(r, p.rows), :] = mask_ref[...]
    field[pl.ds(r + p.rows, r), :] = halo[1]

    for step in range(ITERS):
        low = field[...].astype(jnp.bfloat16).astype(jnp.float32)
        for q in range(p.stretches):
            blocks = []
            for b in range(q * p.per, min((q + 1) * p.per, p.side)):
                moved = shifted(low, r - b)
                blocks.append(jnp.concatenate(
                    [moved[g * r : g * r + p.window] for g in range(p.groups)], axis=1))
            gap = LANES - len(blocks) * p.window
            blocks.append(jnp.zeros((gap, p.groups * p.width), jnp.float32))
            patches[pl.ds(q * LANES, LANES), :] = jnp.concatenate(blocks, axis=0).astype(jnp.bfloat16)

        for s in range(p.slots):
            rows = pl.ds(s * p.slot_rows, p.slot_rows)
            image = jnp.dot(big[rows, :].astype(jnp.bfloat16), patches[...],
                            preferred_element_type=jnp.float32)
            image = image.reshape(p.channels, r, p.groups * p.width)
            weights = [weight_ref[corners[s], k] for k in range(kinds)]
            intensity = jnp.zeros((r, p.groups * p.width), jnp.float32)
            for j in range(p.channels):
                intensity = intensity + weights[j % kinds] * (image[j] * image[j])
            resist = jax.nn.sigmoid(STEEPNESS * (intensity - THRESHOLD))
            slope = 2.0 * (resist - target) * STEEPNESS * resist * (1.0 - resist)
            slope = jnp.where(s < count, slope, 0.0)
            scaled = [(2.0 * weights[k]) * slope for k in range(kinds)]
            sent = jnp.stack([scaled[j % kinds] * image[j] for j in range(p.channels)])
            source[rows, :] = sent.reshape(p.slot_rows, p.groups * p.width).astype(jnp.bfloat16)

        spread = jnp.dot(big_t[pl.ds(0, p.used), :], source[...], preferred_element_type=jnp.float32)
        sums = jnp.zeros((p.ext, p.width), jnp.float32)
        for b in range(p.side):
            block = spread[p.offset(b) : p.offset(b) + p.window]
            joined = 0.0
            for g in range(p.groups):
                piece = block[:, g * p.width : (g + 1) * p.width]
                parts = []
                if g:
                    parts.append(jnp.zeros((g * r, p.width), jnp.float32))
                parts.append(piece)
                tail = p.ext - p.window - g * r
                if tail:
                    parts.append(jnp.zeros((tail, p.width), jnp.float32))
                joined = joined + jnp.concatenate(parts, axis=0)
            sums = sums + shifted(joined, b - r)
        total[step] = sums

        half = p.ext // 2
        if step < ITERS - 1:
            pair = copies(step + 1, total.at[step, pl.ds(0, half)], total.at[step, pl.ds(half, half)],
                          got.at[step, 0], got.at[step, 1])
            start(pair)
            finish(pair)
            gradient = sums + jnp.concatenate([got[step, 0], got[step, 1]], axis=0)
            after = field[...] - STEP_RATE * gradient
            row = lax.broadcasted_iota(jnp.int32, after.shape, 0)
            inside = ((row >= r) | has_up) & ((row < p.ext - r) | has_down)
            field[...] = jnp.where(inside, after, 0.0)
        else:
            pair = copies(step + 1, total.at[step, pl.ds(0, r)], total.at[step, pl.ds(p.ext - r, r)],
                          got.at[step, 0, pl.ds(half - r, r)], got.at[step, 1, pl.ds(0, r)])
            start(pair)
            finish(pair)
            outer = jnp.concatenate([got[step, 0, pl.ds(half - r, r)], got[step, 1, pl.ds(0, r)]], axis=0)
            own = sums[r : r + p.rows]
            out_ref[...] = field[pl.ds(r, p.rows), :] - STEP_RATE * (own + outer)


def laid_out(kernels, p):
    corners, channels, side, _ = kernels.shape
    value = jnp.swapaxes(kernels, 2, 3).astype(jnp.float32)
    value = jnp.pad(value, ((0, 0), (0, 0), (0, p.stretches * p.per - side), (0, p.window - side)))
    value = value.reshape(corners, channels, p.stretches, p.per * p.window)
    value = jnp.pad(value, ((0, 0), (0, 0), (0, 0), (0, LANES - p.per * p.window)))
    return value.reshape(corners, channels, p.depth)


def body(devices, mask, target, kernels, corner_weights, hotspots, counts):
    rows, width = mask.shape
    p = Plan(rows, width, kernels.shape[1], kernels.shape[-1], hotspots.shape[1])
    assert rows == 2 * p.radius and p.radius == 8
    base = laid_out(kernels, p)
    smem = pl.BlockSpec(memory_space=pltpu.SMEM)
    vmem = pl.BlockSpec(memory_space=pltpu.VMEM)
    wide = p.groups * width
    return pl.pallas_call(
        functools.partial(kernel, p, devices),
        out_shape=jax.ShapeDtypeStruct((rows, width), jnp.float32),
        in_specs=[smem, smem, smem, vmem, vmem, vmem],
        out_specs=vmem,
        scratch_shapes=[
            pltpu.VMEM((p.mix, p.depth), jnp.float32),
            pltpu.VMEM((p.depth, p.mix), jnp.bfloat16),
            pltpu.VMEM((p.depth, wide), jnp.bfloat16),
            pltpu.VMEM((p.mix, wide), jnp.bfloat16),
            pltpu.VMEM((p.ext, width), jnp.float32),
            pltpu.VMEM((ITERS, p.ext, width), jnp.float32),
            pltpu.VMEM((2, p.radius, width), jnp.float32),
            pltpu.VMEM((ITERS, 2, p.ext // 2, width), jnp.float32),
            pltpu.SemaphoreType.DMA((ITERS + 1, 2)),
            pltpu.SemaphoreType.DMA((ITERS + 1, 2)),
        ],
        compiler_params=pltpu.CompilerParams(collective_id=0, has_side_effects=True),
        name="litho",
    )(hotspots, counts, corner_weights, mask, target, base)


def solution(mesh):
    placed = (
        P(("strip", "row"), None),
        P(("strip", "row"), None),
        P(),
        P(),
        P("strip", None),
        P("strip"),
    )
    return jax.shard_map(
        functools.partial(body, mesh.shape["row"]), mesh=mesh, in_specs=placed,
        out_specs=P(("strip", "row"), None), check_vma=False
    )
```

```python
import functools

import jax
import jax.numpy as jnp
from jax import lax
from jax.experimental import pallas as pl
from jax.experimental.pallas import tpu as pltpu
from jax.sharding import PartitionSpec as P

ITERS = 2
STEEPNESS = 4.0
THRESHOLD = 0.8
STEP_RATE = 1.0
LANES = 128
MESH = pl.DeviceIdType.MESH


def cdiv(a, b):
    return -(-a // b)


def round_up(a, b):
    return cdiv(a, b) * b


class Plan:
    def __init__(self, rows, width, channels, side, slots):
        self.rows, self.width, self.channels = rows, width, channels
        self.side, self.slots = side, slots
        self.radius = side // 2
        self.groups = rows // self.radius
        self.ext = rows + 2 * self.radius
        self.window = 3 * self.radius
        self.per = LANES // self.window
        self.stretches = cdiv(side, self.per)
        self.depth = self.stretches * LANES
        self.block = round_up(side * self.radius, 16)
        self.lane_step = 32
        self.packed = cdiv(side * self.lane_step, LANES) * LANES
        self.slot_rows = channels * self.radius
        self.mix = round_up(slots * self.slot_rows, 256)

    def offset(self, b):
        return (b // self.per) * LANES + (b % self.per) * self.window


def shifted(value, by):
    width = value.shape[1]
    if by == 0:
        return value
    moved = pltpu.roll(value, by % width, 1)
    column = lax.broadcasted_iota(jnp.int32, value.shape, 1)
    keep = column >= by if by > 0 else column < width + by
    return jnp.where(keep, moved, 0.0)


def kernel(p, devices, hot_ref, count_ref, weight_ref, mask_ref, target_ref, taps_hbm, out_ref,
           taps, pack, big, big_low, big_t, patches, source, field, total, halo, got,
           load_sem, send_sem, recv_sem):
    me = lax.axis_index("row")
    r = p.radius
    has_up, has_down = me > 0, me < devices - 1
    kinds = weight_ref.shape[1]

    load = pltpu.make_async_copy(taps_hbm, taps, load_sem)
    load.start()
    barrier = pltpu.get_barrier_semaphore()

    @pl.when(has_up)
    def _():
        pl.semaphore_signal(barrier, inc=1, device_id={"row": me - 1}, device_id_type=MESH)

    @pl.when(has_down)
    def _():
        pl.semaphore_signal(barrier, inc=1, device_id={"row": me + 1}, device_id_type=MESH)

    def copies(stage, up_src, down_src, above, below):
        up = pltpu.make_async_remote_copy(
            src_ref=up_src, dst_ref=below, send_sem=send_sem.at[stage, 0],
            recv_sem=recv_sem.at[stage, 0], device_id={"row": me - 1}, device_id_type=MESH)
        down = pltpu.make_async_remote_copy(
            src_ref=down_src, dst_ref=above, send_sem=send_sem.at[stage, 1],
            recv_sem=recv_sem.at[stage, 1], device_id={"row": me + 1}, device_id_type=MESH)
        return up, down

    def start(pair):
        up, down = pair

        @pl.when(has_up)
        def _():
            up.start()

        @pl.when(has_down)
        def _():
            down.start()

    def finish(pair):
        up, down = pair

        @pl.when(has_up)
        def _():
            up.wait_send()
            down.wait_recv()

        @pl.when(has_down)
        def _():
            down.wait_send()
            up.wait_recv()

    @pl.when(jnp.logical_not(has_up))
    def _():
        halo[0] = jnp.zeros(halo.shape[1:], halo.dtype)
        for step in range(ITERS):
            got[step, 0] = jnp.zeros(got.shape[2:], got.dtype)

    @pl.when(jnp.logical_not(has_down))
    def _():
        halo[1] = jnp.zeros(halo.shape[1:], halo.dtype)
        for step in range(ITERS):
            got[step, 1] = jnp.zeros(got.shape[2:], got.dtype)

    shape = (p.packed, p.depth)
    spot = lax.broadcasted_iota(jnp.int32, (1, p.depth), 1)
    inside = spot & (LANES - 1)
    nth = jnp.zeros_like(spot)
    for k in range(1, p.per + 1):
        nth = nth + (inside >= k * p.window).astype(jnp.int32)
    tap_row = inside - nth * p.window
    tap_col = (spot // LANES) * p.per + nth
    valid = (nth < p.per) & (tap_row < p.side) & (tap_col < p.side)
    wanted = jnp.where(valid, tap_row * p.lane_step + tap_col, -1)
    place = (lax.broadcasted_iota(jnp.int32, shape, 0) == wanted).astype(jnp.float32).astype(jnp.bfloat16)

    corners = [hot_ref[s, me] for s in range(p.slots)]
    count = count_ref[me]
    pack[...] = jnp.zeros(pack.shape, jnp.float32)
    load.wait()
    for s in range(p.slots):
        for a in range(p.side):
            pack[pl.ds(s * p.channels, p.channels), pl.ds(a * p.lane_step, p.side)] = (
                taps[corners[s], a].astype(jnp.float32))

    inner = has_up & has_down

    @pl.when(inner)
    def _():
        pl.semaphore_wait(barrier, 2)

    @pl.when(jnp.logical_not(inner))
    def _():
        pl.semaphore_wait(barrier, 1)

    first = copies(0, mask_ref.at[pl.ds(0, r)], mask_ref.at[pl.ds(p.rows - r, r)],
                   halo.at[0], halo.at[1])
    start(first)

    base = jnp.dot(pack[...].astype(jnp.bfloat16), place, preferred_element_type=jnp.float32)
    for s in range(p.slots):
        for q in range(p.stretches):
            part = base[s * p.channels : (s + 1) * p.channels, q * LANES : (q + 1) * LANES]
            wide = jnp.broadcast_to(part[:, None, :], (p.channels, r, LANES))
            turned = pltpu.roll(wide, 0, 2, stride=1, stride_axis=1)
            flat = turned.reshape(p.slot_rows, LANES)
            where = (pl.ds(s * p.slot_rows, p.slot_rows), pl.ds(q * LANES, LANES))
            big[where] = flat
            big_low[where] = flat.astype(jnp.bfloat16)
    rest = p.mix - p.slots * p.slot_rows
    if rest:
        big[pl.ds(p.slots * p.slot_rows, rest), :] = jnp.zeros((rest, p.depth), jnp.float32)
        source[pl.ds(p.slots * p.slot_rows, rest), :] = jnp.zeros((rest, source.shape[1]), jnp.bfloat16)
    for q in range(p.mix // 256):
        turned = big[pl.ds(q * 256, 256), :].T
        rows = []
        for third in range(p.window // r):
            for b in range(p.side):
                at = p.offset(b) + third * r
                rows.append(turned[at : at + r])
            spare = p.block - p.side * r
            if spare:
                rows.append(jnp.zeros((spare, 256), jnp.float32))
        big_t[:, pl.ds(q * 256, 256)] = jnp.concatenate(rows, axis=0).astype(jnp.bfloat16)

    target = jnp.concatenate([target_ref[pl.ds(g * r, r), :] for g in range(p.groups)], axis=1)
    finish(first)
    field[pl.ds(0, r), :] = halo[0]
    field[pl.ds(r, p.rows), :] = mask_ref[...]
    field[pl.ds(r + p.rows, r), :] = halo[1]

    for step in range(ITERS):
        low = field[...].astype(jnp.bfloat16).astype(jnp.float32)
        for q in range(p.stretches):
            blocks = []
            for b in range(q * p.per, min((q + 1) * p.per, p.side)):
                moved = shifted(low, r - b)
                blocks.append(jnp.concatenate(
                    [moved[g * r : g * r + p.window] for g in range(p.groups)], axis=1))
            gap = LANES - len(blocks) * p.window
            blocks.append(jnp.zeros((gap, p.groups * p.width), jnp.float32))
            patches[pl.ds(q * LANES, LANES), :] = jnp.concatenate(blocks, axis=0).astype(jnp.bfloat16)

        for s in range(p.slots):
            rows = pl.ds(s * p.slot_rows, p.slot_rows)
            image = jnp.dot(big_low[rows, :], patches[...],
                            preferred_element_type=jnp.float32)
            image = image.reshape(p.channels, r, p.groups * p.width)
            weights = [weight_ref[corners[s], k] for k in range(kinds)]
            intensity = jnp.zeros((r, p.groups * p.width), jnp.float32)
            for j in range(p.channels):
                intensity = intensity + weights[j % kinds] * (image[j] * image[j])
            resist = jax.nn.sigmoid(STEEPNESS * (intensity - THRESHOLD))
            slope = 2.0 * (resist - target) * STEEPNESS * resist * (1.0 - resist)
            slope = jnp.where(s < count, slope, 0.0)
            scaled = [(2.0 * weights[k]) * slope for k in range(kinds)]
            sent = jnp.stack([scaled[j % kinds] * image[j] for j in range(p.channels)])
            source[rows, :] = sent.reshape(p.slot_rows, p.groups * p.width).astype(jnp.bfloat16)

        def spread(third, thirds, group):
            return jnp.dot(big_t[pl.ds(third * p.block, thirds * p.block), :],
                           source[:, pl.ds(group * p.width, p.width)], preferred_element_type=jnp.float32)

        def summed(value, thirds):
            sums = jnp.zeros((thirds * r, p.width), jnp.float32)
            for b in range(p.side):
                rows = [value[k * p.block + b * r : k * p.block + (b + 1) * r] for k in range(thirds)]
                sums = sums + shifted(rows[0] if thirds == 1 else jnp.concatenate(rows, axis=0), b - r)
            return sums

        total[step, pl.ds(0, r), :] = summed(spread(0, 1, 0), 1)
        total[step, pl.ds(r + p.rows, r), :] = summed(spread(2, 1, 1), 1)
        edges = copies(2 * step + 1, total.at[step, pl.ds(0, r)], total.at[step, pl.ds(r + p.rows, r)],
                       got.at[step, 0, pl.ds(r, r)], got.at[step, 1, pl.ds(0, r)])
        start(edges)
        own = summed(spread(1, 2, 0) + spread(0, 2, 1), 2)
        if step < ITERS - 1:
            total[step, pl.ds(r, p.rows), :] = own
            pair = copies(2 * step + 2, total.at[step, pl.ds(r, r)], total.at[step, pl.ds(p.rows, r)],
                          got.at[step, 0, pl.ds(0, r)], got.at[step, 1, pl.ds(r, r)])
            start(pair)
            finish(edges)
            finish(pair)
            gradient = total[step] + jnp.concatenate([got[step, 0], got[step, 1]], axis=0)
            after = field[...] - STEP_RATE * gradient
            row = lax.broadcasted_iota(jnp.int32, after.shape, 0)
            kept = ((row >= r) | has_up) & ((row < p.ext - r) | has_down)
            field[...] = jnp.where(kept, after, 0.0)
        else:
            before = field[pl.ds(r, p.rows), :]
            finish(edges)
            outer = jnp.concatenate([got[step, 0, pl.ds(r, r)], got[step, 1, pl.ds(0, r)]], axis=0)
            out_ref[...] = before - STEP_RATE * (own + outer)


def body(devices, mask, target, kernels, corner_weights, hotspots, counts):
    rows, width = mask.shape
    p = Plan(rows, width, kernels.shape[1], kernels.shape[-1], hotspots.shape[1])
    assert rows == 2 * p.radius and p.radius == 8
    taps = jnp.transpose(kernels, (0, 2, 1, 3))
    smem = pl.BlockSpec(memory_space=pltpu.SMEM)
    vmem = pl.BlockSpec(memory_space=pltpu.VMEM)
    wide = p.groups * width
    return pl.pallas_call(
        functools.partial(kernel, p, devices),
        out_shape=jax.ShapeDtypeStruct((rows, width), jnp.float32),
        in_specs=[smem, smem, smem, vmem, vmem, pl.BlockSpec(memory_space=pl.ANY)],
        out_specs=vmem,
        scratch_shapes=[
            pltpu.VMEM(taps.shape, taps.dtype),
            pltpu.VMEM((p.slots * p.channels, p.packed), jnp.float32),
            pltpu.VMEM((p.mix, p.depth), jnp.float32),
            pltpu.VMEM((p.slots * p.slot_rows, p.depth), jnp.bfloat16),
            pltpu.VMEM((p.window // p.radius * p.block, p.mix), jnp.bfloat16),
            pltpu.VMEM((p.depth, wide), jnp.bfloat16),
            pltpu.VMEM((p.mix, wide), jnp.bfloat16),
            pltpu.VMEM((p.ext, width), jnp.float32),
            pltpu.VMEM((ITERS, p.ext, width), jnp.float32),
            pltpu.VMEM((2, p.radius, width), jnp.float32),
            pltpu.VMEM((ITERS, 2, p.ext // 2, width), jnp.float32),
            pltpu.SemaphoreType.DMA,
            pltpu.SemaphoreType.DMA((2 * ITERS, 2)),
            pltpu.SemaphoreType.DMA((2 * ITERS, 2)),
        ],
        compiler_params=pltpu.CompilerParams(collective_id=0, has_side_effects=True),
        name="litho",
    )(hotspots.T, counts, corner_weights, mask, target, taps)


def solution(mesh):
    placed = (
        P(("strip", "row"), None),
        P(("strip", "row"), None),
        P(),
        P(),
        P("strip", None),
        P("strip"),
    )
    return jax.shard_map(
        functools.partial(body, mesh.shape["row"]), mesh=mesh, in_specs=placed,
        out_specs=P(("strip", "row"), None), check_vma=False
    )
```

```python
import functools

import jax
import jax.numpy as jnp
from jax import lax
from jax.experimental import pallas as pl
from jax.experimental.pallas import tpu as pltpu
from jax.sharding import PartitionSpec as P

ITERS = 2
STEEPNESS = 4.0
THRESHOLD = 0.8
STEP_RATE = 1.0
LANES = 128
MESH = pl.DeviceIdType.MESH


def cdiv(a, b):
    return -(-a // b)


def round_up(a, b):
    return cdiv(a, b) * b


class Plan:
    def __init__(self, rows, width, channels, side, slots):
        self.rows, self.width, self.channels = rows, width, channels
        self.side, self.slots = side, slots
        self.radius = side // 2
        self.groups = rows // self.radius
        self.ext = rows + 2 * self.radius
        self.window = 3 * self.radius
        self.per = LANES // self.window
        self.stretches = cdiv(side, self.per)
        self.depth = self.stretches * LANES
        self.block = round_up(side * self.radius, 16)
        self.lane_step = 32
        self.packed = cdiv(side * self.lane_step, LANES) * LANES
        self.slot_rows = channels * self.radius
        self.mix = round_up(slots * self.slot_rows, 256)

    def offset(self, b):
        return (b // self.per) * LANES + (b % self.per) * self.window


def shifted(value, by):
    width = value.shape[1]
    if by == 0:
        return value
    moved = pltpu.roll(value, by % width, 1)
    column = lax.broadcasted_iota(jnp.int32, value.shape, 1)
    keep = column >= by if by > 0 else column < width + by
    return jnp.where(keep, moved, 0.0)


def kernel(p, devices, hot_hbm, count_hbm, weight_hbm, mask_hbm, target_hbm, taps_hbm, out_ref,
           hot_ref, count_ref, weight_ref, target_ref, taps, pack, big, big_low, big_t, patches,
           source, field, total, got, load_sem, send_sem, recv_sem):
    me = lax.axis_index("row")
    r = p.radius
    has_up, has_down = me > 0, me < devices - 1
    kinds = weight_hbm.shape[1]

    barrier = pltpu.get_barrier_semaphore()

    @pl.when(has_up)
    def _():
        pl.semaphore_signal(barrier, inc=1, device_id={"row": me - 1}, device_id_type=MESH)

    @pl.when(has_down)
    def _():
        pl.semaphore_signal(barrier, inc=1, device_id={"row": me + 1}, device_id_type=MESH)

    pairs = ((taps_hbm, taps), (hot_hbm, hot_ref), (count_hbm, count_ref), (weight_hbm, weight_ref),
             (target_hbm, target_ref), (mask_hbm, field.at[pl.ds(r, p.rows)]))
    loads = [pltpu.make_async_copy(a, b, load_sem.at[k]) for k, (a, b) in enumerate(pairs)]
    for load in loads:
        load.start()

    def copies(stage, up_src, down_src, above, below):
        up = pltpu.make_async_remote_copy(
            src_ref=up_src, dst_ref=below, send_sem=send_sem.at[stage, 0],
            recv_sem=recv_sem.at[stage, 0], device_id={"row": me - 1}, device_id_type=MESH)
        down = pltpu.make_async_remote_copy(
            src_ref=down_src, dst_ref=above, send_sem=send_sem.at[stage, 1],
            recv_sem=recv_sem.at[stage, 1], device_id={"row": me + 1}, device_id_type=MESH)
        return up, down

    def start(pair):
        up, down = pair

        @pl.when(has_up)
        def _():
            up.start()

        @pl.when(has_down)
        def _():
            down.start()

    def finish(pair):
        up, down = pair

        @pl.when(has_up)
        def _():
            up.wait_send()
            down.wait_recv()

        @pl.when(has_down)
        def _():
            down.wait_send()
            up.wait_recv()

    @pl.when(jnp.logical_not(has_up))
    def _():
        field[pl.ds(0, r), :] = jnp.zeros((r, p.width), field.dtype)
        for step in range(ITERS):
            got[step, 0] = jnp.zeros(got.shape[2:], got.dtype)

    @pl.when(jnp.logical_not(has_down))
    def _():
        field[pl.ds(r + p.rows, r), :] = jnp.zeros((r, p.width), field.dtype)
        for step in range(ITERS):
            got[step, 1] = jnp.zeros(got.shape[2:], got.dtype)

    shape = (p.packed, p.depth)
    spot = lax.broadcasted_iota(jnp.int32, (1, p.depth), 1)
    inside = spot & (LANES - 1)
    nth = jnp.zeros_like(spot)
    for k in range(1, p.per + 1):
        nth = nth + (inside >= k * p.window).astype(jnp.int32)
    tap_row = inside - nth * p.window
    tap_col = (spot // LANES) * p.per + nth
    valid = (nth < p.per) & (tap_row < p.side) & (tap_col < p.side)
    wanted = jnp.where(valid, tap_row * p.lane_step + tap_col, -1)
    place = (lax.broadcasted_iota(jnp.int32, shape, 0) == wanted).astype(jnp.float32).astype(jnp.bfloat16)

    pack[...] = jnp.zeros(pack.shape, jnp.float32)
    inner = has_up & has_down

    @pl.when(inner)
    def _():
        pl.semaphore_wait(barrier, 2)

    @pl.when(jnp.logical_not(inner))
    def _():
        pl.semaphore_wait(barrier, 1)

    first = copies(0, mask_hbm.at[pl.ds(0, r)], mask_hbm.at[pl.ds(p.rows - r, r)],
                   field.at[pl.ds(0, r)], field.at[pl.ds(r + p.rows, r)])
    start(first)

    for load in loads:
        load.wait()
    corners = [hot_ref[s, me] for s in range(p.slots)]
    count = count_ref[me]
    for s in range(p.slots):
        for a in range(p.side):
            pack[pl.ds(s * p.channels, p.channels), pl.ds(a * p.lane_step, p.side)] = (
                taps[corners[s], a].astype(jnp.float32))

    base = jnp.dot(pack[...].astype(jnp.bfloat16), place, preferred_element_type=jnp.float32)
    for s in range(p.slots):
        for q in range(p.stretches):
            part = base[s * p.channels : (s + 1) * p.channels, q * LANES : (q + 1) * LANES]
            wide = jnp.broadcast_to(part[:, None, :], (p.channels, r, LANES))
            turned = pltpu.roll(wide, 0, 2, stride=1, stride_axis=1)
            flat = turned.reshape(p.slot_rows, LANES)
            where = (pl.ds(s * p.slot_rows, p.slot_rows), pl.ds(q * LANES, LANES))
            big[where] = flat
            big_low[where] = flat.astype(jnp.bfloat16)
    rest = p.mix - p.slots * p.slot_rows
    if rest:
        big[pl.ds(p.slots * p.slot_rows, rest), :] = jnp.zeros((rest, p.depth), jnp.float32)
        source[pl.ds(p.slots * p.slot_rows, rest), :] = jnp.zeros((rest, source.shape[1]), jnp.bfloat16)
    for q in range(p.mix // 256):
        turned = big[pl.ds(q * 256, 256), :].T
        rows = []
        for third in range(p.window // r):
            for b in range(p.side):
                at = p.offset(b) + third * r
                rows.append(turned[at : at + r])
            spare = p.block - p.side * r
            if spare:
                rows.append(jnp.zeros((spare, 256), jnp.float32))
        big_t[:, pl.ds(q * 256, 256)] = jnp.concatenate(rows, axis=0).astype(jnp.bfloat16)

    target = jnp.concatenate([target_ref[pl.ds(g * r, r), :] for g in range(p.groups)], axis=1)
    finish(first)

    for step in range(ITERS):
        low = field[...].astype(jnp.bfloat16).astype(jnp.float32)
        for q in range(p.stretches):
            blocks = []
            for b in range(q * p.per, min((q + 1) * p.per, p.side)):
                moved = shifted(low, r - b)
                blocks.append(jnp.concatenate(
                    [moved[g * r : g * r + p.window] for g in range(p.groups)], axis=1))
            gap = LANES - len(blocks) * p.window
            blocks.append(jnp.zeros((gap, p.groups * p.width), jnp.float32))
            patches[pl.ds(q * LANES, LANES), :] = jnp.concatenate(blocks, axis=0).astype(jnp.bfloat16)

        for s in range(p.slots):
            rows = pl.ds(s * p.slot_rows, p.slot_rows)
            image = jnp.dot(big_low[rows, :], patches[...],
                            preferred_element_type=jnp.float32)
            image = image.reshape(p.channels, r, p.groups * p.width)
            weights = [weight_ref[corners[s], k] for k in range(kinds)]
            intensity = jnp.zeros((r, p.groups * p.width), jnp.float32)
            for j in range(p.channels):
                intensity = intensity + weights[j % kinds] * (image[j] * image[j])
            resist = jax.nn.sigmoid(STEEPNESS * (intensity - THRESHOLD))
            slope = 2.0 * (resist - target) * STEEPNESS * resist * (1.0 - resist)
            slope = jnp.where(s < count, slope, 0.0)
            scaled = [(2.0 * weights[k]) * slope for k in range(kinds)]
            sent = jnp.stack([scaled[j % kinds] * image[j] for j in range(p.channels)])
            source[rows, :] = sent.reshape(p.slot_rows, p.groups * p.width).astype(jnp.bfloat16)

        def spread(third, thirds, group):
            return jnp.dot(big_t[pl.ds(third * p.block, thirds * p.block), :],
                           source[:, pl.ds(group * p.width, p.width)], preferred_element_type=jnp.float32)

        def summed(value, thirds):
            sums = jnp.zeros((thirds * r, p.width), jnp.float32)
            for b in range(p.side):
                rows = [value[k * p.block + b * r : k * p.block + (b + 1) * r] for k in range(thirds)]
                sums = sums + shifted(rows[0] if thirds == 1 else jnp.concatenate(rows, axis=0), b - r)
            return sums

        total[step, pl.ds(0, r), :] = summed(spread(0, 1, 0), 1)
        total[step, pl.ds(r + p.rows, r), :] = summed(spread(2, 1, 1), 1)
        edges = copies(2 * step + 1, total.at[step, pl.ds(0, r)], total.at[step, pl.ds(r + p.rows, r)],
                       got.at[step, 0, pl.ds(r, r)], got.at[step, 1, pl.ds(0, r)])
        start(edges)
        own = summed(spread(1, 2, 0) + spread(0, 2, 1), 2)
        if step < ITERS - 1:
            total[step, pl.ds(r, p.rows), :] = own
            pair = copies(2 * step + 2, total.at[step, pl.ds(r, r)], total.at[step, pl.ds(p.rows, r)],
                          got.at[step, 0, pl.ds(0, r)], got.at[step, 1, pl.ds(r, r)])
            start(pair)
            finish(edges)
            finish(pair)
            gradient = total[step] + jnp.concatenate([got[step, 0], got[step, 1]], axis=0)
            after = field[...] - STEP_RATE * gradient
            row = lax.broadcasted_iota(jnp.int32, after.shape, 0)
            kept = ((row >= r) | has_up) & ((row < p.ext - r) | has_down)
            field[...] = jnp.where(kept, after, 0.0)
        else:
            before = field[pl.ds(r, p.rows), :]
            finish(edges)
            outer = jnp.concatenate([got[step, 0, pl.ds(r, r)], got[step, 1, pl.ds(0, r)]], axis=0)
            out_ref[...] = before - STEP_RATE * (own + outer)


def body(devices, mask, target, kernels, corner_weights, hotspots, counts):
    rows, width = mask.shape
    p = Plan(rows, width, kernels.shape[1], kernels.shape[-1], hotspots.shape[1])
    assert rows == 2 * p.radius and p.radius == 8
    taps = jnp.transpose(kernels, (0, 2, 1, 3))
    vmem = pl.BlockSpec(memory_space=pltpu.VMEM)
    wide = p.groups * width
    return pl.pallas_call(
        functools.partial(kernel, p, devices),
        out_shape=pltpu.VMEM((rows, width), jnp.float32),
        in_specs=[pl.BlockSpec(memory_space=pl.ANY)] * 6,
        out_specs=vmem,
        scratch_shapes=[
            pltpu.SMEM(hotspots.shape[::-1], hotspots.dtype),
            pltpu.SMEM(counts.shape, counts.dtype),
            pltpu.SMEM(corner_weights.shape, corner_weights.dtype),
            pltpu.VMEM(target.shape, target.dtype),
            pltpu.VMEM(taps.shape, taps.dtype),
            pltpu.VMEM((p.slots * p.channels, p.packed), jnp.float32),
            pltpu.VMEM((p.mix, p.depth), jnp.float32),
            pltpu.VMEM((p.slots * p.slot_rows, p.depth), jnp.bfloat16),
            pltpu.VMEM((p.window // p.radius * p.block, p.mix), jnp.bfloat16),
            pltpu.VMEM((p.depth, wide), jnp.bfloat16),
            pltpu.VMEM((p.mix, wide), jnp.bfloat16),
            pltpu.VMEM((p.ext, width), jnp.float32),
            pltpu.VMEM((ITERS, p.ext, width), jnp.float32),
            pltpu.VMEM((ITERS, 2, p.ext // 2, width), jnp.float32),
            pltpu.SemaphoreType.DMA((6,)),
            pltpu.SemaphoreType.DMA((2 * ITERS, 2)),
            pltpu.SemaphoreType.DMA((2 * ITERS, 2)),
        ],
        compiler_params=pltpu.CompilerParams(collective_id=0, has_side_effects=True),
        name="litho",
    )(hotspots.T, counts, corner_weights, mask, target, taps)


def solution(mesh):
    placed = (
        P(("strip", "row"), None),
        P(("strip", "row"), None),
        P(),
        P(),
        P("strip", None),
        P("strip"),
    )
    return jax.shard_map(
        functools.partial(body, mesh.shape["row"]), mesh=mesh, in_specs=placed,
        out_specs=P(("strip", "row"), None), check_vma=False
    )
```
